32 devices in a mesh: expert: 8 (over z, y), replica: 4 (over x, core).
Axes of the slice: x: 2, y: 2, z: 4, core: 2. Of those that a mesh axis runs over, the one named last changes fastest.
Arguments:
- tokens: bfloat16 [4096, 2048], P(('expert', 'replica')), may hold values from -6 to 6
- out_grad: bfloat16 [4096, 2048], P(('expert', 'replica')), may hold values from -6 to 6
- expert_ids: int32 [4096, 2], P(('expert', 'replica')), may hold values from 0 to 3, as said below
- route_weights: bfloat16 [4096, 2], P(('expert', 'replica')), may hold values from 0.25 to 1
- capacity: int32 [4], replicated, may hold values from 2 to 2
- w_gate: bfloat16 [8, 2048, 384], P('expert', 'replica'), may hold values from -0.125 to 0.125
- w_up: bfloat16 [8, 2048, 384], P('expert', 'replica'), may hold values from -0.125 to 0.125
- w_down: bfloat16 [8, 384, 2048], P('expert', None, 'replica'), may hold values from -0.21875 to 0.21875
Outputs:
- x_grad: bfloat16 [4096, 2048], P(('expert', 'replica'))
- gate_grad: bfloat16 [8, 2048, 384], P('expert', 'replica')
- up_grad: bfloat16 [8, 2048, 384], P('expert', 'replica')
- down_grad: bfloat16 [8, 384, 2048], P('expert')
The draws below stay inside these ranges and needn't reach their ends.
Inputs may be any that keep to these rules, and one draw needn't show every extreme that they name: `expert_ids`: each row names 2 different experts.
All inputs are finite; a program needn't handle non-finite values.
Results may differ from the reference program's by a relative error of at most 0.009.
Values may be sent and summed in bfloat16 or wider, within the bound.
A program may use at most 64 MiB of HBM per device.

```python
import jax
import jax.numpy as jnp
from jax import lax

D = 2048
H = 768
HALF = 384
EXPERTS = 4
TOP = 2
TOK_DEV = 128
CAP = 2
TOKENS = 4096
N_EXPERT = 8
N_REPLICA = 4


def hot_expert(key):
    return jax.random.randint(jax.random.fold_in(key, 11), (), 0, EXPERTS)


def draw_expert_ids(key, part):
    hot = hot_expert(key)
    blocks = TOKENS // TOK_DEV
    hot_rows = max(CAP, min(TOK_DEV, 3 * TOK_DEV * TOP // EXPERTS))
    first, second, third, fourth = jax.random.split(jax.random.fold_in(key, 12), 4)
    expert_range = jnp.arange(EXPERTS, dtype=jnp.int32)
    bias = jax.random.randint(first, (EXPERTS,), 0, 4)
    noise = jax.random.randint(second, (blocks, TOK_DEV, EXPERTS), 0, 1024)
    scores = (noise + 40 * bias[None, None, :]) * EXPERTS + expert_range[None, None, :]
    scores = jnp.where(expert_range[None, None, :] == hot, -1, scores)
    picked = lax.top_k(scores, TOP)[1].astype(jnp.int32)
    order = jax.random.randint(third, (blocks, TOK_DEV), 0, 1048576) * TOK_DEV + jnp.arange(TOK_DEV, dtype=jnp.int32)[None, :]
    rank = jnp.argsort(jnp.argsort(order, axis=1), axis=1)
    is_hot = rank < hot_rows
    picked = picked.at[:, :, TOP - 1].set(jnp.where(is_hot, hot, picked[:, :, TOP - 1]))
    shift = jax.random.randint(fourth, (blocks, TOK_DEV, 1), 0, TOP)
    turn = (jnp.arange(TOP, dtype=jnp.int32)[None, None, :] + shift) % TOP
    picked = jnp.take_along_axis(picked, turn, axis=2)
    return picked.reshape(TOKENS, TOP).astype(jnp.int32)


def draw_capacity(key, part):
    hot = hot_expert(key)
    values = jax.random.randint(jax.random.fold_in(key, 13), (EXPERTS,), max(2, CAP // 2), CAP + 1)
    return jnp.where(jnp.arange(EXPERTS, dtype=jnp.int32) == hot, CAP, values).astype(jnp.int32)


def levels(key, dims, cuts, least, high):
    loudness, own = 1.0, jax.random.fold_in(key, 6)
    for position, shards_of in cuts:
        steps = jnp.exp(jax.random.uniform(jax.random.fold_in(own, position), (shards_of,), jnp.float32, least / len(cuts), high / len(cuts)))
        loudness = loudness * jnp.repeat(steps, dims[position] // shards_of).reshape([-1 if axis == position else 1 for axis in range(len(dims))])
    return loudness


def normal_values(own_key, dims, scale, most, pieces=(), kind=jnp.bfloat16):
    array = scale * jax.random.normal(own_key, dims, jnp.float32)
    if pieces:
        array = array * levels(own_key, dims, pieces, -0.22, 0.18)
    return jnp.clip(array, -most, most).astype(kind)


def setup_inputs(seed: int = 0) -> dict:
    key_list = jax.random.split(jax.random.key(seed), 9)
    return {
        "tokens": normal_values(key_list[0], (TOKENS, D), 1.0, 6.0, ((0, 32),)),
        "out_grad": normal_values(key_list[1], (TOKENS, D), 1.0, 6.0, ((0, 32),)),
        "expert_ids": draw_expert_ids(jax.random.fold_in(key_list[8], 71), 0),
        "route_weights": jnp.clip(0.25 + 0.75 * jax.random.uniform(key_list[3], (TOKENS, TOP), jnp.float32) ** levels(key_list[3], (TOKENS, TOP), ((0, 32),), -0.2, 0.2), 0.25, 1.0).astype(jnp.bfloat16),
        "capacity": draw_capacity(jax.random.fold_in(key_list[8], 71), 0),
        "w_gate": normal_values(key_list[5], (N_EXPERT, D, HALF), D ** -0.5, 0.125, ((0, 8), (1, 4))),
        "w_up": normal_values(key_list[6], (N_EXPERT, D, HALF), D ** -0.5, 0.125, ((0, 8), (1, 4))),
        "w_down": normal_values(key_list[7], (N_EXPERT, HALF, D), H ** -0.5, 0.21875, ((0, 8), (2, 4))),
    }


def regroup(values):
    return jnp.swapaxes(values.reshape(N_EXPERT, N_REPLICA, CAP, values.shape[-1]), 0, 1).reshape(N_REPLICA, N_EXPERT * CAP, values.shape[-1])


def replica_total(parts):
    rounded = lax.optimization_barrier(parts.astype(jnp.bfloat16))
    return jnp.sum(rounded.astype(jnp.float32), axis=0).astype(jnp.bfloat16)


def reference(tokens, out_grad, expert_ids, route_weights, capacity, w_gate, w_up, w_down):
    blocks = TOKENS // TOK_DEV
    expert_range = jnp.arange(EXPERTS, dtype=jnp.int32)
    chosen = (expert_ids[:, :, None] == expert_range[None, None, :]).astype(jnp.int32)
    per_row = jnp.sum(chosen, axis=1).reshape(blocks, TOK_DEV, EXPERTS)
    ranks = jnp.cumsum(per_row, axis=1).reshape(TOKENS, EXPERTS)
    place = jnp.sum(chosen * ranks[:, None, :], axis=2) - 1
    limit = jnp.sum(chosen * capacity[None, None, :], axis=2)
    kept = place < limit
    block_of = (jnp.arange(TOKENS, dtype=jnp.int32) // TOK_DEV)[:, None]
    dump = EXPERTS * blocks * CAP
    index = jnp.where(kept, (expert_ids * blocks + block_of) * CAP + place, dump).reshape(-1)
    row_ids = jnp.broadcast_to(jnp.arange(TOKENS, dtype=jnp.int32)[:, None], (TOKENS, TOP)).reshape(-1)
    rows_of = jnp.full((dump + 1,), TOKENS, jnp.int32).at[index].set(row_ids)
    weight_of = jnp.zeros((dump + 1,), jnp.float32).at[index].set(route_weights.astype(jnp.float32).reshape(-1))
    rows_of = rows_of[:-1].reshape(EXPERTS, blocks * CAP)
    weight_of = weight_of[:-1].reshape(EXPERTS, blocks * CAP)
    padded_x = jnp.concatenate([tokens, jnp.zeros((1, D), tokens.dtype)], axis=0)
    padded_dy = jnp.concatenate([out_grad, jnp.zeros((1, D), out_grad.dtype)], axis=0)
    gate_full = jnp.transpose(w_gate.reshape(EXPERTS, 2, D, HALF), (0, 2, 1, 3)).reshape(EXPERTS, D, H)
    up_full = jnp.transpose(w_up.reshape(EXPERTS, 2, D, HALF), (0, 2, 1, 3)).reshape(EXPERTS, D, H)
    down_full = w_down.reshape(EXPERTS, H, D)

    def step(carry, item):
        rows, weights, gate_mat, up_mat, down_mat = item
        inputs = padded_x[rows]
        cotangent = padded_dy[rows]
        gate = jnp.dot(inputs, gate_mat, preferred_element_type=jnp.float32)
        up = jnp.dot(inputs, up_mat, preferred_element_type=jnp.float32)
        sig = jax.nn.sigmoid(gate)
        act = gate * sig
        hidden = (act * up).astype(jnp.bfloat16)
        scaled = (weights[:, None] * cotangent.astype(jnp.float32)).astype(jnp.bfloat16)
        back = jnp.dot(scaled, down_mat.T, preferred_element_type=jnp.float32)
        gate_back = (back * up * sig * (1.0 + gate * (1.0 - sig))).astype(jnp.bfloat16)
        up_back = (back * act).astype(jnp.bfloat16)
        slot_total = jnp.zeros((rows.shape[0], D), jnp.float32)
        for half in range(2):
            lo = half * HALF
            hi = lo + HALF
            part = jnp.dot(gate_back[:, lo:hi], gate_mat[:, lo:hi].T, preferred_element_type=jnp.float32)
            part = part + jnp.dot(up_back[:, lo:hi], up_mat[:, lo:hi].T, preferred_element_type=jnp.float32)
            rounded = lax.optimization_barrier(part.astype(jnp.bfloat16))
            slot_total = slot_total + rounded.astype(jnp.float32)
        carry = carry.at[rows].add(slot_total)
        grouped_x = regroup(inputs).astype(jnp.float32)
        gate_parts = jnp.einsum('rnd,rnh->rdh', grouped_x, regroup(gate_back).astype(jnp.float32))
        up_parts = jnp.einsum('rnd,rnh->rdh', grouped_x, regroup(up_back).astype(jnp.float32))
        down_parts = jnp.einsum('rnh,rnd->rhd', regroup(hidden).astype(jnp.float32), regroup(scaled).astype(jnp.float32))
        return carry, (replica_total(gate_parts), replica_total(up_parts), replica_total(down_parts))

    start = jnp.zeros((TOKENS + 1, D), jnp.float32)
    total, grads = lax.scan(step, start, (rows_of, weight_of, gate_full, up_full, down_full))
    x_grad = total[:TOKENS].astype(jnp.bfloat16)
    gate_grad = jnp.transpose(grads[0].reshape(EXPERTS, D, 2, HALF), (0, 2, 1, 3)).reshape(N_EXPERT, D, HALF)
    up_grad = jnp.transpose(grads[1].reshape(EXPERTS, D, 2, HALF), (0, 2, 1, 3)).reshape(N_EXPERT, D, HALF)
    down_grad = grads[2].reshape(N_EXPERT, HALF, D)
    return x_grad, gate_grad, up_grad, down_grad
```

```python
import functools

import jax
import jax.numpy as jnp
from jax import lax
from jax.experimental import pallas as pl
from jax.experimental.pallas import tpu as pltpu
from jax.sharding import PartitionSpec as P

CAP = 2
F32, BF16 = jnp.float32, jnp.bfloat16


def dot(a, b, dims):
    return lax.dot_general(a, b, (dims, ((), ())), preferred_element_type=F32)


def kernel(
    n, reps, ids_ref, rw_ref, cap_ref, tok_ref, og_ref, wg_hbm, wu_hbm, wd_hbm,
    xg_ref, gg_ref, ug_ref, dg_ref,
    wg_ref, wu_ref, wd_ref, send, recv, cots, part, got1, got2, grads, rsend, rrecv,
    wsem, lsem, ssem, rsem,
):
    total = n * reps
    mo, mr = lax.axis_index("expert"), lax.axis_index("replica")
    me = mo * reps + mr
    core, pair = lax.rem(mr, 2), lax.div(mr, 2)
    block, width = tok_ref.shape
    dr = width // reps
    half = wg_ref.shape[1]
    slots = n * CAP
    rows = total * CAP

    def remote(src, dst, k, o, r):
        return pltpu.make_async_remote_copy(
            src_ref=src, dst_ref=dst, send_sem=ssem.at[k], recv_sem=rsem.at[k],
            device_id={"expert": o, "replica": r}, device_id_type=pl.DeviceIdType.MESH,
        )

    def where(k):
        g = lax.rem(me + k, total)
        return g, lax.div(g, reps), lax.rem(g, reps)

    loads = [
        pltpu.make_async_copy(src, dst, wsem.at[i])
        for i, (src, dst) in enumerate(((wg_hbm, wg_ref), (wu_hbm, wu_ref), (wd_hbm, wd_ref)))
    ]
    for load in loads:
        load.start()

    barrier = pltpu.get_barrier_semaphore()

    @pl.loop(1, total)
    def _(k):
        _, o, r = where(k)
        pl.semaphore_signal(
            barrier, inc=1, device_id={"expert": o, "replica": r},
            device_id_type=pl.DeviceIdType.MESH,
        )

    column = lax.broadcasted_iota(jnp.int32, (block, slots), 1)
    expert = column // (2 * CAP)
    place = column % CAP
    limit = jnp.zeros((block, slots), jnp.int32)
    for e in range(cap_ref.shape[0]):
        limit = jnp.where(expert == e, cap_ref[e], limit)
    named = jnp.zeros((block, slots), F32)
    weight = jnp.zeros((block, slots), F32)
    for k in range(ids_ref.shape[1]):
        hit = ids_ref[:, k : k + 1] == expert
        named = named + jnp.where(hit, 1.0, 0.0)
        weight = weight + jnp.where(hit, rw_ref[:, k : k + 1].astype(F32), 0.0)
    lower = jnp.where(
        lax.broadcasted_iota(jnp.int32, (block, block), 0)
        >= lax.broadcasted_iota(jnp.int32, (block, block), 1),
        1.0, 0.0,
    ).astype(BF16)
    ranks = dot(lower, named.astype(BF16), ((1,), (0,)))
    kept = (named > 0.0) & (ranks == (place + 1).astype(F32)) & (place < limit)
    picker = jnp.where(kept, 1.0, 0.0)
    slot_weight = dot(
        (picker * weight).astype(BF16), jnp.ones((block, 128), BF16), ((0,), (0,))
    )[:, :1]
    picker = picker.astype(BF16)
    for r in range(reps):
        cols = pl.ds(r * dr, dr)
        picked = dot(picker, tok_ref[:, cols], ((0,), (0,)))
        scaled = dot(picker, og_ref[:, cols], ((0,), (0,))) * slot_weight
        send[:, r, 0] = picked.reshape(n, CAP, dr).astype(BF16)
        send[:, r, 1] = scaled.reshape(n, CAP, dr).astype(BF16)

    pl.semaphore_wait(barrier, total - 1)

    own = pltpu.make_async_copy(send.at[mo, mr], recv.at[:, me], lsem.at[0])
    own.start()

    @pl.loop(1, total)
    def _(k):
        _, o, r = where(k)
        remote(send.at[o, r], recv.at[:, me], 0, o, r).start()

    for load in loads:
        load.wait()
    own.wait()
    arrived = recv.at[:, pl.ds(0, total - 1)]
    pltpu.make_async_copy(arrived, arrived, rsem.at[0]).wait()

    inputs = recv[0].astype(F32).reshape(rows, dr).astype(BF16)
    cot = recv[1].astype(F32).reshape(rows, dr).astype(BF16)
    wg, wu, wd = wg_ref[...], wu_ref[...], wd_ref[...]
    part[:, :, :half] = dot(inputs, wg, ((1,), (0,))).reshape(2, rows // 2, half)
    part[:, :, half : 2 * half] = dot(inputs, wu, ((1,), (0,))).reshape(2, rows // 2, half)
    part[:, :, 2 * half :] = dot(cot, wd, ((1,), (1,))).reshape(2, rows // 2, half)
    mate = lax.bitwise_xor(mr, 1)
    first = remote(part.at[1 - core], got1, 1, mo, mate)
    first.start()
    first.wait()

    got2[pair] = (part[core] + got1[...]).astype(BF16)
    pairs = reps // 2
    second = []
    for k in range(1, pairs):
        to = lax.rem(pair + k, pairs) * 2 + core
        second.append(remote(got2.at[pair], got2.at[pair], 1 + k, mo, to))
        second[-1].start()
    for copy in second:
        copy.wait()

    spread = []
    for k in range(1, reps):
        to = lax.rem(mr + k, reps)
        spread.append(remote(recv.at[1], cots.at[mr], 1 + pairs + k, mo, to))
        spread[-1].start()

    summed = got2[0].astype(F32)
    for k in range(1, pairs):
        summed = summed + got2[k].astype(F32)
    gate, up, back = summed[:, :half], summed[:, half : 2 * half], summed[:, 2 * half :]
    sig = jax.nn.sigmoid(gate)
    act = gate * sig
    grads[core, :, :half] = (back * up * sig * (1.0 + gate * (1.0 - sig))).astype(BF16)
    grads[core, :, half : 2 * half] = (back * act).astype(BF16)
    grads[core, :, 2 * half :] = (act * up).astype(BF16)
    third = remote(grads.at[core], grads.at[core], 1 + pairs, mo, mate)
    third.start()
    third.wait()

    both = grads[...].reshape(rows, 3 * half)
    gate_back, up_back, hidden = both[:, :half], both[:, half : 2 * half], both[:, 2 * half :]
    result = dot(gate_back, wg, ((1,), (1,))) + dot(up_back, wu, ((1,), (1,)))
    rsend[...] = result.reshape(total, CAP, dr).astype(BF16)

    back_own = pltpu.make_async_copy(rsend.at[me], rrecv.at[mo, mr], lsem.at[1])
    back_own.start()
    ret = 1 + pairs + reps

    @pl.loop(1, total)
    def _(k):
        g, o, r = where(k)
        remote(rsend.at[g], rrecv.at[mo, mr], ret, o, r).start()

    gg_ref[...] = dot(inputs, gate_back, ((0,), (0,))).astype(BF16)
    ug_ref[...] = dot(inputs, up_back, ((0,), (0,))).astype(BF16)
    for copy in spread:
        copy.wait()
    cots[mr] = recv[1]
    for r in range(reps):
        c = cots[r].astype(F32).reshape(rows, dr).astype(BF16)
        dg_ref[:, pl.ds(r * dr, dr)] = dot(hidden, c, ((0,), (0,))).astype(BF16)

    back_own.wait()
    returned = rsend.at[pl.ds(0, total - 1)]
    pltpu.make_async_copy(returned, returned, rsem.at[ret]).wait()
    for r in range(reps):
        rows_r = rrecv[:, r].astype(F32).reshape(slots, dr).astype(BF16)
        xg_ref[:, pl.ds(r * dr, dr)] = dot(picker, rows_r, ((1,), (0,))).astype(BF16)
    pltpu.make_async_copy(arrived, arrived, ssem.at[0]).wait()
    pltpu.make_async_copy(returned, returned, ssem.at[ret]).wait()


def shards(n, reps, tokens, out_grad, expert_ids, route_weights, capacity, w_gate, w_up, w_down):
    block, width = tokens.shape
    dr, half = w_gate.shape[1:]
    total = n * reps
    rows = total * CAP
    sems = 2 + reps // 2 + reps
    vmem = pl.BlockSpec(memory_space=pltpu.VMEM)
    hbm = pl.BlockSpec(memory_space=pl.ANY)
    x_grad, gate_grad, up_grad, down_grad = pl.pallas_call(
        functools.partial(kernel, n, reps),
        out_shape=(
            jax.ShapeDtypeStruct((block, width), BF16),
            jax.ShapeDtypeStruct((dr, half), BF16),
            jax.ShapeDtypeStruct((dr, half), BF16),
            jax.ShapeDtypeStruct((half, width), BF16),
        ),
        in_specs=[vmem, vmem, pl.BlockSpec(memory_space=pltpu.SMEM), vmem, vmem, hbm, hbm, hbm],
        out_specs=(vmem,) * 4,
        scratch_shapes=[
            pltpu.VMEM((dr, half), BF16),
            pltpu.VMEM((dr, half), BF16),
            pltpu.VMEM((half, dr), BF16),
            pltpu.VMEM((n, reps, 2, CAP, dr), BF16),
            pltpu.VMEM((2, total, CAP, dr), BF16),
            pltpu.VMEM((reps, total, CAP, dr), BF16),
            pltpu.VMEM((2, rows // 2, 3 * half), F32),
            pltpu.VMEM((rows // 2, 3 * half), F32),
            pltpu.VMEM((reps // 2, rows // 2, 3 * half), BF16),
            pltpu.VMEM((2, rows // 2, 3 * half), BF16),
            pltpu.VMEM((total, CAP, dr), BF16),
            pltpu.VMEM((n, reps, CAP, dr), BF16),
            pltpu.SemaphoreType.DMA((3,)),
            pltpu.SemaphoreType.DMA((2,)),
            pltpu.SemaphoreType.DMA((sems,)),
            pltpu.SemaphoreType.DMA((sems,)),
        ],
        compiler_params=pltpu.CompilerParams(collective_id=0, has_side_effects=True),
    )(
        expert_ids, route_weights, capacity, tokens, out_grad,
        w_gate.reshape(dr, half), w_up.reshape(dr, half), w_down.reshape(half, dr),
    )
    return x_grad, gate_grad[None], up_grad[None], down_grad[None]


def solution(mesh):
    return jax.shard_map(
        functools.partial(shards, mesh.shape["expert"], mesh.shape["replica"]),
        mesh=mesh,
        in_specs=(
            P(("expert", "replica"), None),
            P(("expert", "replica"), None),
            P(("expert", "replica"), None),
            P(("expert", "replica"), None),
            P(),
            P("expert", "replica", None),
            P("expert", "replica", None),
            P("expert", None, "replica"),
        ),
        out_specs=(
            P(("expert", "replica"), None),
            P("expert", "replica", None),
            P("expert", "replica", None),
            P("expert", None, None),
        ),
        check_vma=False,
    )
```

```python
import functools

import jax
import jax.numpy as jnp
from jax import lax
from jax.experimental import pallas as pl
from jax.experimental.pallas import tpu as pltpu
from jax.sharding import PartitionSpec as P

CAP = 2
F32, BF16 = jnp.float32, jnp.bfloat16


def dot(a, b, dims):
    return lax.dot_general(a, b, (dims, ((), ())), preferred_element_type=F32)


def kernel(
    n, reps, ids_ref, rw_ref, cap_ref, tok_hbm, og_hbm, wg_hbm, wu_hbm, wd_hbm,
    pick_ref, back_ref, gg_ref, ug_ref, dg_ref,
    tok_ref, og_ref, wg_ref, wu_ref, wd_ref, send, recv, cots, part, got1, got2, grads,
    rsend, rrecv, wsem, lsem, ssem, rsem,
):
    total = n * reps
    mo, mr = lax.axis_index("expert"), lax.axis_index("replica")
    me = mo * reps + mr
    core, pair = lax.rem(mr, 2), lax.div(mr, 2)
    block, width = tok_ref.shape
    dr = width // reps
    half = wg_ref.shape[1]
    slots = n * CAP
    rows = total * CAP
    pairs = reps // 2

    def remote(src, dst, k, o, r):
        return pltpu.make_async_remote_copy(
            src_ref=src, dst_ref=dst, send_sem=ssem.at[k], recv_sem=rsem.at[k],
            device_id={"expert": o, "replica": r}, device_id_type=pl.DeviceIdType.MESH,
        )

    def where(k):
        g = lax.rem(me + k, total)
        return g, lax.div(g, reps), lax.rem(g, reps)

    loads = [
        pltpu.make_async_copy(src, dst, wsem.at[i])
        for i, (src, dst) in enumerate((
            (tok_hbm, tok_ref), (og_hbm, og_ref),
            (wg_hbm, wg_ref), (wu_hbm, wu_ref), (wd_hbm, wd_ref),
        ))
    ]
    for load in loads:
        load.start()

    barrier = pltpu.get_barrier_semaphore()

    @pl.loop(1, total)
    def _(k):
        _, o, r = where(k)
        pl.semaphore_signal(
            barrier, inc=1, device_id={"expert": o, "replica": r},
            device_id_type=pl.DeviceIdType.MESH,
        )

    row = lax.broadcasted_iota(jnp.int32, (slots, block), 0)
    expert = row // (2 * CAP)
    place = row % CAP
    limit = jnp.zeros((slots, block), jnp.int32)
    for e in range(cap_ref.shape[0]):
        limit = jnp.where(expert == e, cap_ref[e], limit)
    named = jnp.zeros((slots, block), F32)
    weight = jnp.zeros((slots, block), F32)
    for k in range(ids_ref.shape[0]):
        hit = ids_ref[k : k + 1, :] == expert
        named = named + jnp.where(hit, 1.0, 0.0)
        weight = weight + jnp.where(hit, rw_ref[k : k + 1, :].astype(F32), 0.0)
    upper = jnp.where(
        lax.broadcasted_iota(jnp.int32, (block, block), 0)
        <= lax.broadcasted_iota(jnp.int32, (block, block), 1),
        1.0, 0.0,
    ).astype(BF16)
    ranks = dot(named.astype(BF16), upper, ((1,), (0,)))
    kept = (named > 0.0) & (ranks == (place + 1).astype(F32)) & (place < limit)
    picker = jnp.where(kept, 1.0, 0.0)
    slot_weight = jnp.sum(picker * weight, axis=1, keepdims=True)
    picker = picker.astype(BF16)
    pick_ref[...] = picker
    loads[0].wait()
    loads[1].wait()
    for r in range(reps):
        cols = pl.ds(r * dr, dr)
        picked = dot(picker, tok_ref[:, cols], ((1,), (0,)))
        scaled = dot(picker, og_ref[:, cols], ((1,), (0,))) * slot_weight
        send[:, r, 0] = picked.reshape(n, CAP, dr).astype(BF16)
        send[:, r, 1] = scaled.reshape(n, CAP, dr).astype(BF16)

    pl.semaphore_wait(barrier, total - 1)

    own = pltpu.make_async_copy(send.at[mo, mr], recv.at[:, me], lsem.at[0])
    own.start()

    @pl.loop(1, total)
    def _(k):
        _, o, r = where(k)
        remote(send.at[o, r], recv.at[:, me], 0, o, r).start()

    for load in loads[2:]:
        load.wait()
    own.wait()
    arrived = recv.at[:, pl.ds(0, total - 1)]
    pltpu.make_async_copy(arrived, arrived, rsem.at[0]).wait()

    mate = lax.bitwise_xor(mr, 1)
    peers = [lax.rem(pair + k, pairs) * 2 + core for k in range(1, pairs)]
    across = [
        remote(recv.at[1], cots.at[mr], 2 + pairs + k, mo, to) for k, to in enumerate(peers)
    ]
    for copy in across:
        copy.start()

    inputs = recv[0].astype(F32).reshape(rows, dr).astype(BF16)
    cot = recv[1].astype(F32).reshape(rows, dr).astype(BF16)
    wg, wu, wd = wg_ref[...], wu_ref[...], wd_ref[...]
    part[:, :, :half] = dot(inputs, wg, ((1,), (0,))).reshape(2, rows // 2, half)
    part[:, :, half : 2 * half] = dot(inputs, wu, ((1,), (0,))).reshape(2, rows // 2, half)
    part[:, :, 2 * half :] = dot(cot, wd, ((1,), (1,))).reshape(2, rows // 2, half)
    first = remote(part.at[1 - core], got1, 1, mo, mate)
    first.start()
    first.wait()

    got2[pair] = (part[core] + got1[...]).astype(BF16)
    second = [remote(got2.at[pair], got2.at[pair], 2 + k, mo, to) for k, to in enumerate(peers)]
    for copy in second:
        copy.start()
    for copy in second:
        copy.wait()

    summed = got2[0].astype(F32)
    for k in range(1, pairs):
        summed = summed + got2[k].astype(F32)
    gate, up, back = summed[:, :half], summed[:, half : 2 * half], summed[:, 2 * half :]
    sig = jax.nn.sigmoid(gate)
    act = gate * sig
    grads[core, :, :half] = (back * up * sig * (1.0 + gate * (1.0 - sig))).astype(BF16)
    grads[core, :, half : 2 * half] = (back * act).astype(BF16)
    grads[core, :, 2 * half :] = (act * up).astype(BF16)
    third = remote(grads.at[core], grads.at[core], 1 + pairs, mo, mate)
    third.start()

    base = 2 + 2 * pairs
    passed = [remote(recv.at[1], cots.at[mr], base, mo, mate)]
    passed[0].start()
    for k in range(1, pairs):
        across[k - 1].wait()
        came = lax.rem(pair + pairs - k, pairs) * 2 + core
        passed.append(remote(cots.at[came], cots.at[came], base + k, mo, mate))
        passed[-1].start()
    third.wait()

    both = grads[...].reshape(rows, 3 * half)
    gate_back, up_back, hidden = both[:, :half], both[:, half : 2 * half], both[:, 2 * half :]
    result = dot(gate_back, wg, ((1,), (1,))) + dot(up_back, wu, ((1,), (1,)))
    rsend[...] = result.reshape(total, CAP, dr).astype(BF16)

    back_own = pltpu.make_async_copy(rsend.at[me], rrecv.at[mo, mr], lsem.at[1])
    back_own.start()
    ret = base + pairs

    @pl.loop(1, total)
    def _(k):
        g, o, r = where(k)
        remote(rsend.at[g], rrecv.at[mo, mr], ret, o, r).start()

    gg_ref[...] = dot(inputs, gate_back, ((0,), (0,))).astype(BF16)
    ug_ref[...] = dot(inputs, up_back, ((0,), (0,))).astype(BF16)
    for copy in passed:
        copy.wait()
    cots[mr] = recv[1]
    for r in range(reps):
        c = cots[r].astype(F32).reshape(rows, dr).astype(BF16)
        dg_ref[:, pl.ds(r * dr, dr)] = dot(hidden, c, ((0,), (0,))).astype(BF16)

    back_own.wait()
    returned = rsend.at[pl.ds(0, total - 1)]
    pltpu.make_async_copy(returned, returned, rsem.at[ret]).wait()
    for r in range(reps):
        back_ref[:, pl.ds(r * dr, dr)] = rrecv[:, r].astype(F32).reshape(slots, dr).astype(BF16)
    pltpu.make_async_copy(arrived, arrived, ssem.at[0]).wait()
    pltpu.make_async_copy(returned, returned, ssem.at[ret]).wait()


def finish(pick_ref, back_ref, gg_in, ug_in, dg_in, xg_out, gg_out, ug_out, dg_out, xg, sem):
    copies = [
        pltpu.make_async_copy(src, dst, sem.at[i])
        for i, (src, dst) in enumerate(
            ((dg_in, dg_out), (gg_in, gg_out), (ug_in, ug_out), (xg, xg_out))
        )
    ]
    for copy in copies[:3]:
        copy.start()
    xg[...] = dot(pick_ref[...], back_ref[...], ((0,), (0,))).astype(BF16)
    copies[3].start()
    for copy in copies:
        copy.wait()


def shards(n, reps, tokens, out_grad, expert_ids, route_weights, capacity, w_gate, w_up, w_down):
    block, width = tokens.shape
    dr, half = w_gate.shape[1:]
    total = n * reps
    rows = total * CAP
    sems = 3 + 3 * (reps // 2)
    vmem = pl.BlockSpec(memory_space=pltpu.VMEM)
    hbm = pl.BlockSpec(memory_space=pl.ANY)
    shapes = ((block, width), (dr, half), (dr, half), (half, width))
    partial = pl.pallas_call(
        functools.partial(kernel, n, reps),
        out_shape=tuple(
            pltpu.VMEM(shape, BF16) for shape in ((n * CAP, block), (n * CAP, width), *shapes[1:])
        ),
        in_specs=[vmem, vmem, pl.BlockSpec(memory_space=pltpu.SMEM)] + [hbm] * 5,
        out_specs=(vmem,) * 5,
        scratch_shapes=[
            pltpu.VMEM((block, width), BF16),
            pltpu.VMEM((block, width), BF16),
            pltpu.VMEM((dr, half), BF16),
            pltpu.VMEM((dr, half), BF16),
            pltpu.VMEM((half, dr), BF16),
            pltpu.VMEM((n, reps, 2, CAP, dr), BF16),
            pltpu.VMEM((2, total, CAP, dr), BF16),
            pltpu.VMEM((reps, total, CAP, dr), BF16),
            pltpu.VMEM((2, rows // 2, 3 * half), F32),
            pltpu.VMEM((rows // 2, 3 * half), F32),
            pltpu.VMEM((reps // 2, rows // 2, 3 * half), BF16),
            pltpu.VMEM((2, rows // 2, 3 * half), BF16),
            pltpu.VMEM((total, CAP, dr), BF16),
            pltpu.VMEM((n, reps, CAP, dr), BF16),
            pltpu.SemaphoreType.DMA((5,)),
            pltpu.SemaphoreType.DMA((2,)),
            pltpu.SemaphoreType.DMA((sems,)),
            pltpu.SemaphoreType.DMA((sems,)),
        ],
        compiler_params=pltpu.CompilerParams(collective_id=0, has_side_effects=True),
    )(
        expert_ids.T, route_weights.T, capacity, tokens, out_grad,
        w_gate.reshape(dr, half), w_up.reshape(dr, half), w_down.reshape(half, dr),
    )
    x_grad, gate_grad, up_grad, down_grad = pl.pallas_call(
        finish,
        out_shape=tuple(jax.ShapeDtypeStruct(shape, BF16) for shape in shapes),
        in_specs=[vmem] * 5,
        out_specs=(hbm,) * 4,
        scratch_shapes=[pltpu.VMEM((block, width), BF16), pltpu.SemaphoreType.DMA((4,))],
    )(*(pltpu.with_memory_space_constraint(p, pltpu.VMEM) for p in partial))
    return x_grad, gate_grad[None], up_grad[None], down_grad[None]


def solution(mesh):
    return jax.shard_map(
        functools.partial(shards, mesh.shape["expert"], mesh.shape["replica"]),
        mesh=mesh,
        in_specs=(
            P(("expert", "replica"), None),
            P(("expert", "replica"), None),
            P(("expert", "replica"), None),
            P(("expert", "replica"), None),
            P(),
            P("expert", "replica", None),
            P("expert", "replica", None),
            P("expert", None, "replica"),
        ),
        out_specs=(
            P(("expert", "replica"), None),
            P("expert", "replica", None),
            P("expert", "replica", None),
            P("expert", None, None),
        ),
        check_vma=False,
    )
```

```python
import functools

import jax
import jax.numpy as jnp
from jax import lax
from jax.experimental import pallas as pl
from jax.experimental.pallas import tpu as pltpu
from jax.sharding import PartitionSpec as P

CAP = 2
F32, BF16 = jnp.float32, jnp.bfloat16


def dot(a, b, dims):
    return lax.dot_general(a, b, (dims, ((), ())), preferred_element_type=F32)


def kernel(
    n, reps, ids_ref, rw_ref, cap_ref, tok_hbm, og_hbm, wg_hbm, wu_hbm, wd_hbm,
    pick_ref, back_ref, gg_ref, ug_ref, dg_ref,
    tok_ref, og_ref, wg_ref, wu_ref, wd_ref, send, recv, xs, cots, sums, grads,
    rsend, rrecv, wsem, lsem, ssem, rsem,
):
    pairs = reps // 2
    sources = n * pairs
    mo, mr = lax.axis_index("expert"), lax.axis_index("replica")
    core, pair = lax.rem(mr, 2), lax.div(mr, 2)
    mate = mr + 1 - 2 * core
    me = mo * pairs + pair
    block, width = tok_ref.shape
    dr, half = wg_hbm.shape
    slots = n * CAP
    rows = sources * CAP
    turn = [lax.rem(pair + k, pairs) for k in range(pairs)]

    def remote(src, dst, k, o, r):
        return pltpu.make_async_remote_copy(
            src_ref=src, dst_ref=dst, send_sem=ssem.at[k], recv_sem=rsem.at[k],
            device_id={"expert": o, "replica": r}, device_id_type=pl.DeviceIdType.MESH,
        )

    def everyone(act):
        @pl.loop(1, n)
        def _(k):
            o = lax.rem(mo + k, n)
            for p in turn:
                act(o, p)

        for p in turn[1:]:
            act(mo, p)

    barrier = pltpu.get_barrier_semaphore()

    def hail(o, r):
        pl.semaphore_signal(
            barrier, inc=1, device_id={"expert": o, "replica": r},
            device_id_type=pl.DeviceIdType.MESH,
        )

    everyone(lambda o, p: hail(o, 2 * p + core))
    hail(mo, mate)

    loads = [
        pltpu.make_async_copy(src, dst, wsem.at[i])
        for i, (src, dst) in enumerate((
            (tok_hbm, tok_ref), (og_hbm, og_ref),
            (wg_hbm, wg_ref.at[core]), (wu_hbm, wu_ref.at[core]), (wd_hbm, wd_ref.at[core]),
        ))
    ]
    for load in loads:
        load.start()

    row = lax.broadcasted_iota(jnp.int32, (slots, block), 0)
    expert = row // (2 * CAP)
    place = row % CAP
    limit = jnp.zeros((slots, block), jnp.int32)
    for e in range(cap_ref.shape[0]):
        limit = jnp.where(expert == e, cap_ref[e], limit)
    named = jnp.zeros((slots, block), F32)
    weight = jnp.zeros((slots, block), F32)
    for k in range(ids_ref.shape[0]):
        hit = ids_ref[k : k + 1, :] == expert
        named = named + jnp.where(hit, 1.0, 0.0)
        weight = weight + jnp.where(hit, rw_ref[k : k + 1, :].astype(F32), 0.0)
    upper = jnp.where(
        lax.broadcasted_iota(jnp.int32, (block, block), 0)
        <= lax.broadcasted_iota(jnp.int32, (block, block), 1),
        1.0, 0.0,
    ).astype(BF16)
    ranks = dot(named.astype(BF16), upper, ((1,), (0,)))
    kept = (named > 0.0) & (ranks == (place + 1).astype(F32)) & (place < limit)
    picker = jnp.where(kept, 1.0, 0.0)
    slot_weight = jnp.sum(picker * weight, axis=1, keepdims=True)
    picker = picker.astype(BF16)
    pick_ref[...] = picker
    loads[0].wait()
    loads[1].wait()
    for r in range(reps):
        cols = pl.ds(r * dr, dr)
        picked = dot(picker, tok_ref[:, cols], ((1,), (0,)))
        scaled = dot(picker, og_ref[:, cols], ((1,), (0,))) * slot_weight
        send[:, r // 2, 0, r % 2] = picked.reshape(n, CAP, dr).astype(BF16)
        send[:, r // 2, 1, r % 2] = scaled.reshape(n, CAP, dr).astype(BF16)

    pl.semaphore_wait(barrier, sources)

    own = pltpu.make_async_copy(send.at[mo, pair], recv.at[:, :, me], lsem.at[0])
    own.start()
    everyone(
        lambda o, p: remote(send.at[o, p], recv.at[:, :, me], 0, o, 2 * p + core).start()
    )

    lent = [
        remote(src, dst.at[core], 2 + i, mo, mate)
        for i, (src, dst) in enumerate(((wg_hbm, wg_ref), (wu_hbm, wu_ref), (wd_hbm, wd_ref)))
    ]
    for copy in lent:
        copy.start()
    for load in loads[2:]:
        load.wait()
    own.wait()
    arrived = recv.at[:, :, pl.ds(0, sources - 1)]
    pltpu.make_async_copy(arrived, arrived, rsem.at[0]).wait()

    used = 5
    across = []
    for k in range(1, pairs):
        across.append(remote(recv.at[1], cots.at[core, pair], used, mo, 2 * turn[k] + core))
        across[-1].start()
        used += 1

    def flat(value):
        return value.astype(F32).reshape(rows, dr).astype(BF16)

    x0, x1 = flat(recv[0, 0]), flat(recv[0, 1])
    c0, c1 = flat(recv[1, 0]), flat(recv[1, 1])
    for copy in lent:
        copy.wait()
    wg, wu, wd = [wg_ref[0], wg_ref[1]], [wu_ref[0], wu_ref[1]], [wd_ref[0], wd_ref[1]]
    crossing = []
    for i in range(3):
        if i < 2:
            w = (wg, wu)[i]
            value = dot(x0, w[0], ((1,), (0,))) + dot(x1, w[1], ((1,), (0,)))
        else:
            value = dot(c0, wd[0], ((1,), (1,))) + dot(c1, wd[1], ((1,), (1,)))
        sums[i, pair] = value.astype(BF16)
        for k in range(1, pairs):
            crossing.append(
                remote(sums.at[i, pair], sums.at[i, pair], used, mo, 2 * turn[k] + core)
            )
            crossing[-1].start()
            used += 1
    for copy in crossing:
        copy.wait()

    def total(i):
        value = sums[i, 0].astype(F32)
        for k in range(1, pairs):
            value = value + sums[i, k].astype(F32)
        return value

    gate, up, back = total(0), total(1), total(2)
    sig = jax.nn.sigmoid(gate)
    act = gate * sig
    gate_back = (back * up * sig * (1.0 + gate * (1.0 - sig))).astype(BF16)
    up_back = (back * act).astype(BF16)
    for s in range(2):
        result = dot(gate_back, wg[s], ((1,), (1,))) + dot(up_back, wu[s], ((1,), (1,)))
        rsend[:, s] = result.reshape(sources, CAP, dr).astype(BF16)
    back_own = pltpu.make_async_copy(rsend.at[me], rrecv.at[mo, pair], lsem.at[1])
    back_own.start()
    everyone(
        lambda o, p: remote(
            rsend.at[o * pairs + p], rrecv.at[mo, pair], 1, o, 2 * p + core
        ).start()
    )

    grads[0, core] = gate_back
    grads[1, core] = up_back
    grads[2, core] = (act * up).astype(BF16)
    swaps = [
        remote(recv.at[0, 1 - core], xs.at[core], used, mo, mate),
        remote(grads.at[:, core], grads.at[:, core], used + 1, mo, mate),
        remote(recv.at[1], cots.at[core, pair], used + 2, mo, mate),
    ]
    for copy in swaps:
        copy.start()
    used += 3
    xs[core] = recv[0, core]
    for k in range(1, pairs):
        across[k - 1].wait()
        came = lax.rem(pair + pairs - k, pairs)
        swaps.append(remote(cots.at[core, came], cots.at[core, came], used, mo, mate))
        swaps[-1].start()
        used += 1
    cots[core, pair] = recv[1]
    for copy in swaps:
        copy.wait()

    inputs = xs[...].astype(F32).reshape(2 * rows, dr).astype(BF16)
    gg_ref[...] = dot(inputs, grads[0].reshape(2 * rows, half), ((0,), (0,))).astype(BF16)
    ug_ref[...] = dot(inputs, grads[1].reshape(2 * rows, half), ((0,), (0,))).astype(BF16)
    hidden = grads[2].reshape(2 * rows, half)
    for r in range(reps):
        c = cots[:, r // 2, r % 2].astype(F32).reshape(2 * rows, dr).astype(BF16)
        dg_ref[:, pl.ds(r * dr, dr)] = dot(hidden, c, ((0,), (0,))).astype(BF16)

    back_own.wait()
    returned = rsend.at[pl.ds(0, sources - 1)]
    pltpu.make_async_copy(returned, returned, rsem.at[1]).wait()
    for r in range(reps):
        parts = rrecv[:, r // 2, r % 2].astype(F32).reshape(slots, dr).astype(BF16)
        back_ref[:, pl.ds(r * dr, dr)] = parts
    pltpu.make_async_copy(arrived, arrived, ssem.at[0]).wait()
    pltpu.make_async_copy(returned, returned, ssem.at[1]).wait()


def finish(pick_ref, back_ref, gg_in, ug_in, dg_in, xg_out, gg_out, ug_out, dg_out, xg, sem):
    copies = [
        pltpu.make_async_copy(src, dst, sem.at[i])
        for i, (src, dst) in enumerate(
            ((dg_in, dg_out), (gg_in, gg_out), (ug_in, ug_out), (xg, xg_out))
        )
    ]
    for copy in copies[:3]:
        copy.start()
    xg[...] = dot(pick_ref[...], back_ref[...], ((0,), (0,))).astype(BF16)
    copies[3].start()
    for copy in copies:
        copy.wait()


def shards(n, reps, tokens, out_grad, expert_ids, route_weights, capacity, w_gate, w_up, w_down):
    block, width = tokens.shape
    dr, half = w_gate.shape[1:]
    pairs = reps // 2
    sources = n * pairs
    rows = sources * CAP
    sems = 8 + 5 * (pairs - 1)
    vmem = pl.BlockSpec(memory_space=pltpu.VMEM)
    hbm = pl.BlockSpec(memory_space=pl.ANY)
    shapes = ((block, width), (dr, half), (dr, half), (half, width))
    partial = pl.pallas_call(
        functools.partial(kernel, n, reps),
        out_shape=tuple(
            pltpu.VMEM(shape, BF16) for shape in ((n * CAP, block), (n * CAP, width), *shapes[1:])
        ),
        in_specs=[vmem, vmem, pl.BlockSpec(memory_space=pltpu.SMEM)] + [hbm] * 5,
        out_specs=(vmem,) * 5,
        scratch_shapes=[
            pltpu.VMEM((block, width), BF16),
            pltpu.VMEM((block, width), BF16),
            pltpu.VMEM((2, dr, half), BF16),
            pltpu.VMEM((2, dr, half), BF16),
            pltpu.VMEM((2, half, dr), BF16),
            pltpu.VMEM((n, pairs, 2, 2, CAP, dr), BF16),
            pltpu.VMEM((2, 2, sources, CAP, dr), BF16),
            pltpu.VMEM((2, sources, CAP, dr), BF16),
            pltpu.VMEM((2, pairs, 2, sources, CAP, dr), BF16),
            pltpu.VMEM((3, pairs, rows, half), BF16),
            pltpu.VMEM((3, 2, rows, half), BF16),
            pltpu.VMEM((sources, 2, CAP, dr), BF16),
            pltpu.VMEM((n, pairs, 2, CAP, dr), BF16),
            pltpu.SemaphoreType.DMA((5,)),
            pltpu.SemaphoreType.DMA((2,)),
            pltpu.SemaphoreType.DMA((sems,)),
            pltpu.SemaphoreType.DMA((sems,)),
        ],
        compiler_params=pltpu.CompilerParams(collective_id=0, has_side_effects=True),
    )(
        expert_ids.T, route_weights.T, capacity, tokens, out_grad,
        w_gate.reshape(dr, half), w_up.reshape(dr, half), w_down.reshape(half, dr),
    )
    x_grad, gate_grad, up_grad, down_grad = pl.pallas_call(
        finish,
        out_shape=tuple(jax.ShapeDtypeStruct(shape, BF16) for shape in shapes),
        in_specs=[vmem] * 5,
        out_specs=(hbm,) * 4,
        scratch_shapes=[pltpu.VMEM((block, width), BF16), pltpu.SemaphoreType.DMA((4,))],
    )(*(pltpu.with_memory_space_constraint(p, pltpu.VMEM) for p in partial))
    return x_grad, gate_grad[None], up_grad[None], down_grad[None]


def solution(mesh):
    return jax.shard_map(
        functools.partial(shards, mesh.shape["expert"], mesh.shape["replica"]),
        mesh=mesh,
        in_specs=(
            P(("expert", "replica"), None),
            P(("expert", "replica"), None),
            P(("expert", "replica"), None),
            P(("expert", "replica"), None),
            P(),
            P("expert", "replica", None),
            P("expert", "replica", None),
            P("expert", None, "replica"),
        ),
        out_specs=(
            P(("expert", "replica"), None),
            P("expert", "replica", None),
            P("expert", "replica", None),
            P("expert", None, None),
        ),
        check_vma=False,
    )
```

```python
import functools

import jax
import jax.numpy as jnp
from jax import lax
from jax.experimental import pallas as pl
from jax.experimental.pallas import tpu as pltpu
from jax.sharding import PartitionSpec as P

CAP = 2
F32, BF16 = jnp.float32, jnp.bfloat16


def dot(a, b, dims):
    return lax.dot_general(a, b, (dims, ((), ())), preferred_element_type=F32)


def kernel(
    n, reps, ids_ref, rw_ref, cap_ref, tok_hbm, og_hbm, wg_hbm, wu_hbm, wd_hbm,
    pick_ref, back_ref, gg_ref, ug_ref, dg_ref,
    tok_ref, og_ref, wg_ref, wu_ref, wd_ref, send, recv, xs, cots, sums, grads,
    rsend, rrecv, wsem, lsem, ssem, rsem,
):
    pairs = reps // 2
    sources = n * pairs
    mo, mr = lax.axis_index("expert"), lax.axis_index("replica")
    core, pair = lax.rem(mr, 2), lax.div(mr, 2)
    mate = mr + 1 - 2 * core
    me = mo * pairs + pair
    block, width = tok_ref.shape
    dr, half = wg_hbm.shape
    slots = n * CAP
    rows = sources * CAP
    turn = [lax.rem(pair + k, pairs) for k in range(pairs)]

    def remote(src, dst, k, o, r):
        return pltpu.make_async_remote_copy(
            src_ref=src, dst_ref=dst, send_sem=ssem.at[k], recv_sem=rsem.at[k],
            device_id={"expert": o, "replica": r}, device_id_type=pl.DeviceIdType.MESH,
        )

    def everyone(act):
        @pl.loop(1, n)
        def _(k):
            o = lax.rem(mo + lax.rem(k + n // 2 - 2 + n - 1, n - 1) + 1, n)
            for p in turn:
                act(o, p)

        for p in turn[1:]:
            act(mo, p)

    barrier = pltpu.get_barrier_semaphore()

    def hail(o, r):
        pl.semaphore_signal(
            barrier, inc=1, device_id={"expert": o, "replica": r},
            device_id_type=pl.DeviceIdType.MESH,
        )

    everyone(lambda o, p: hail(o, 2 * p + core))
    hail(mo, mate)

    loads = [
        pltpu.make_async_copy(src, dst, wsem.at[i])
        for i, (src, dst) in enumerate((
            (tok_hbm, tok_ref), (og_hbm, og_ref),
            (wg_hbm, wg_ref.at[core]), (wu_hbm, wu_ref.at[core]), (wd_hbm, wd_ref.at[core]),
        ))
    ]
    for load in loads:
        load.start()

    row = lax.broadcasted_iota(jnp.int32, (slots, block), 0)
    expert = row // (2 * CAP)
    place = row % CAP
    limit = jnp.zeros((slots, block), jnp.int32)
    for e in range(cap_ref.shape[0]):
        limit = jnp.where(expert == e, cap_ref[e], limit)
    named = jnp.zeros((slots, block), F32)
    weight = jnp.zeros((slots, block), F32)
    for k in range(ids_ref.shape[0]):
        hit = ids_ref[k : k + 1, :] == expert
        named = named + jnp.where(hit, 1.0, 0.0)
        weight = weight + jnp.where(hit, rw_ref[k : k + 1, :].astype(F32), 0.0)
    upper = jnp.where(
        lax.broadcasted_iota(jnp.int32, (block, block), 0)
        <= lax.broadcasted_iota(jnp.int32, (block, block), 1),
        1.0, 0.0,
    ).astype(BF16)
    ranks = dot(named.astype(BF16), upper, ((1,), (0,)))
    kept = (named > 0.0) & (ranks == (place + 1).astype(F32)) & (place < limit)
    picker = jnp.where(kept, 1.0, 0.0)
    slot_weight = jnp.sum(picker * weight, axis=1, keepdims=True)
    picker = picker.astype(BF16)
    pick_ref[...] = picker
    loads[0].wait()
    loads[1].wait()
    for r in range(reps):
        cols = pl.ds(r * dr, dr)
        picked = dot(picker, tok_ref[:, cols], ((1,), (0,)))
        scaled = dot(picker, og_ref[:, cols], ((1,), (0,))) * slot_weight
        send[:, r // 2, 0, r % 2] = picked.reshape(n, CAP, dr).astype(BF16)
        send[:, r // 2, 1, r % 2] = scaled.reshape(n, CAP, dr).astype(BF16)

    pl.semaphore_wait(barrier, sources)

    own = pltpu.make_async_copy(send.at[mo, pair], recv.at[:, :, me], lsem.at[0])
    own.start()
    everyone(
        lambda o, p: remote(send.at[o, p], recv.at[:, :, me], 0, o, 2 * p + core).start()
    )

    lent = [
        remote(src, dst.at[core], 2 + i, mo, mate)
        for i, (src, dst) in enumerate(((wg_hbm, wg_ref), (wu_hbm, wu_ref), (wd_hbm, wd_ref)))
    ]
    for copy in lent:
        copy.start()
    for load in loads[2:]:
        load.wait()
    own.wait()
    arrived = recv.at[:, :, pl.ds(0, sources - 1)]
    pltpu.make_async_copy(arrived, arrived, rsem.at[0]).wait()

    used = 5
    across = []
    for k in range(1, pairs):
        across.append(remote(recv.at[1], cots.at[core, pair], used, mo, 2 * turn[k] + core))
        across[-1].start()
        used += 1

    def flat(value):
        return value.astype(F32).reshape(rows, dr).astype(BF16)

    x0, x1 = flat(recv[0, 0]), flat(recv[0, 1])
    c0, c1 = flat(recv[1, 0]), flat(recv[1, 1])
    for copy in lent:
        copy.wait()
    wg, wu, wd = [wg_ref[0], wg_ref[1]], [wu_ref[0], wu_ref[1]], [wd_ref[0], wd_ref[1]]
    crossing = []
    for i in range(3):
        if i < 2:
            w = (wg, wu)[i]
            value = dot(x0, w[0], ((1,), (0,))) + dot(x1, w[1], ((1,), (0,)))
        else:
            value = dot(c0, wd[0], ((1,), (1,))) + dot(c1, wd[1], ((1,), (1,)))
        sums[i, pair] = value.astype(BF16)
        for k in range(1, pairs):
            crossing.append(
                remote(sums.at[i, pair], sums.at[i, pair], used, mo, 2 * turn[k] + core)
            )
            crossing[-1].start()
            used += 1
    for copy in crossing:
        copy.wait()

    def total(i):
        value = sums[i, 0].astype(F32)
        for k in range(1, pairs):
            value = value + sums[i, k].astype(F32)
        return value

    gate, up, back = total(0), total(1), total(2)
    sig = jax.nn.sigmoid(gate)
    act = gate * sig
    gate_back = (back * up * sig * (1.0 + gate * (1.0 - sig))).astype(BF16)
    up_back = (back * act).astype(BF16)
    for s in range(2):
        result = dot(gate_back, wg[s], ((1,), (1,))) + dot(up_back, wu[s], ((1,), (1,)))
        rsend[:, s] = result.reshape(sources, CAP, dr).astype(BF16)
    back_own = pltpu.make_async_copy(rsend.at[me], rrecv.at[mo, pair], lsem.at[1])
    back_own.start()
    everyone(
        lambda o, p: remote(
            rsend.at[o * pairs + p], rrecv.at[mo, pair], 1, o, 2 * p + core
        ).start()
    )

    grads[0, core] = gate_back
    grads[1, core] = up_back
    grads[2, core] = (act * up).astype(BF16)
    swaps = [
        remote(recv.at[0, 1 - core], xs.at[core], used, mo, mate),
        remote(grads.at[:, core], grads.at[:, core], used + 1, mo, mate),
        remote(recv.at[1], cots.at[core, pair], used + 2, mo, mate),
    ]
    for copy in swaps:
        copy.start()
    used += 3
    xs[core] = recv[0, core]
    for k in range(1, pairs):
        across[k - 1].wait()
        came = lax.rem(pair + pairs - k, pairs)
        swaps.append(remote(cots.at[core, came], cots.at[core, came], used, mo, mate))
        swaps[-1].start()
        used += 1
    cots[core, pair] = recv[1]
    for copy in swaps:
        copy.wait()

    inputs = xs[...].astype(F32).reshape(2 * rows, dr).astype(BF16)
    gg_ref[...] = dot(inputs, grads[0].reshape(2 * rows, half), ((0,), (0,))).astype(BF16)
    ug_ref[...] = dot(inputs, grads[1].reshape(2 * rows, half), ((0,), (0,))).astype(BF16)
    hidden = grads[2].reshape(2 * rows, half)
    for r in range(reps):
        c = cots[:, r // 2, r % 2].astype(F32).reshape(2 * rows, dr).astype(BF16)
        dg_ref[:, pl.ds(r * dr, dr)] = dot(hidden, c, ((0,), (0,))).astype(BF16)

    back_own.wait()
    returned = rsend.at[pl.ds(0, sources - 1)]
    pltpu.make_async_copy(returned, returned, rsem.at[1]).wait()
    for r in range(reps):
        parts = rrecv[:, r // 2, r % 2].astype(F32).reshape(slots, dr).astype(BF16)
        back_ref[:, pl.ds(r * dr, dr)] = parts
    pltpu.make_async_copy(arrived, arrived, ssem.at[0]).wait()
    pltpu.make_async_copy(returned, returned, ssem.at[1]).wait()


def finish(pick_ref, back_ref, gg_in, ug_in, dg_in, xg_out, gg_out, ug_out, dg_out, xg, sem):
    copies = [
        pltpu.make_async_copy(src, dst, sem.at[i])
        for i, (src, dst) in enumerate(
            ((dg_in, dg_out), (gg_in, gg_out), (ug_in, ug_out), (xg, xg_out))
        )
    ]
    for copy in copies[:3]:
        copy.start()
    xg[...] = dot(pick_ref[...], back_ref[...], ((0,), (0,))).astype(BF16)
    copies[3].start()
    for copy in copies:
        copy.wait()


def shards(n, reps, tokens, out_grad, expert_ids, route_weights, capacity, w_gate, w_up, w_down):
    block, width = tokens.shape
    dr, half = w_gate.shape[1:]
    pairs = reps // 2
    sources = n * pairs
    rows = sources * CAP
    sems = 8 + 5 * (pairs - 1)
    vmem = pl.BlockSpec(memory_space=pltpu.VMEM)
    hbm = pl.BlockSpec(memory_space=pl.ANY)
    shapes = ((block, width), (dr, half), (dr, half), (half, width))
    partial = pl.pallas_call(
        functools.partial(kernel, n, reps),
        out_shape=tuple(
            pltpu.VMEM(shape, BF16) for shape in ((n * CAP, block), (n * CAP, width), *shapes[1:])
        ),
        in_specs=[vmem, vmem, pl.BlockSpec(memory_space=pltpu.SMEM)] + [hbm] * 5,
        out_specs=(vmem,) * 5,
        scratch_shapes=[
            pltpu.VMEM((block, width), BF16),
            pltpu.VMEM((block, width), BF16),
            pltpu.VMEM((2, dr, half), BF16),
            pltpu.VMEM((2, dr, half), BF16),
            pltpu.VMEM((2, half, dr), BF16),
            pltpu.VMEM((n, pairs, 2, 2, CAP, dr), BF16),
            pltpu.VMEM((2, 2, sources, CAP, dr), BF16),
            pltpu.VMEM((2, sources, CAP, dr), BF16),
            pltpu.VMEM((2, pairs, 2, sources, CAP, dr), BF16),
            pltpu.VMEM((3, pairs, rows, half), BF16),
            pltpu.VMEM((3, 2, rows, half), BF16),
            pltpu.VMEM((sources, 2, CAP, dr), BF16),
            pltpu.VMEM((n, pairs, 2, CAP, dr), BF16),
            pltpu.SemaphoreType.DMA((5,)),
            pltpu.SemaphoreType.DMA((2,)),
            pltpu.SemaphoreType.DMA((sems,)),
            pltpu.SemaphoreType.DMA((sems,)),
        ],
        compiler_params=pltpu.CompilerParams(collective_id=0, has_side_effects=True),
    )(
        expert_ids.T, route_weights.T, capacity, tokens, out_grad,
        w_gate.reshape(dr, half), w_up.reshape(dr, half), w_down.reshape(half, dr),
    )
    x_grad, gate_grad, up_grad, down_grad = pl.pallas_call(
        finish,
        out_shape=tuple(jax.ShapeDtypeStruct(shape, BF16) for shape in shapes),
        in_specs=[vmem] * 5,
        out_specs=(hbm,) * 4,
        scratch_shapes=[pltpu.VMEM((block, width), BF16), pltpu.SemaphoreType.DMA((4,))],
    )(*(pltpu.with_memory_space_constraint(p, pltpu.VMEM) for p in partial))
    return x_grad, gate_grad[None], up_grad[None], down_grad[None]


def solution(mesh):
    return jax.shard_map(
        functools.partial(shards, mesh.shape["expert"], mesh.shape["replica"]),
        mesh=mesh,
        in_specs=(
            P(("expert", "replica"), None),
            P(("expert", "replica"), None),
            P(("expert", "replica"), None),
            P(("expert", "replica"), None),
            P(),
            P("expert", "replica", None),
            P("expert", "replica", None),
            P("expert", None, "replica"),
        ),
        out_specs=(
            P(("expert", "replica"), None),
            P("expert", "replica", None),
            P("expert", "replica", None),
            P("expert", None, None),
        ),
        check_vma=False,
    )
```

```python
import functools

import jax
import jax.numpy as jnp
from jax import lax
from jax.experimental import pallas as pl
from jax.experimental.pallas import tpu as pltpu
from jax.sharding import PartitionSpec as P

CAP = 2
F32, BF16 = jnp.float32, jnp.bfloat16


def dot(a, b, dims):
    return lax.dot_general(a, b, (dims, ((), ())), preferred_element_type=F32)


def kernel(
    n, reps, ids_ref, rw_ref, cap_ref, tok_hbm, og_hbm, wg_hbm, wu_hbm, wd_hbm,
    pick_ref, back_ref, gg_ref, ug_ref, dg_ref,
    tok_ref, og_ref, wg_ref, wu_ref, wd_ref, send, recv, xs, cots, sums, grads,
    rsend, rrecv, wsem, lsem, ssem, rsem,
):
    pairs = reps // 2
    sources = n * pairs
    mo, mr = lax.axis_index("expert"), lax.axis_index("replica")
    core, pair = lax.rem(mr, 2), lax.div(mr, 2)
    mate = mr + 1 - 2 * core
    me = mo * pairs + pair
    block, width = tok_ref.shape
    dr, half = wg_hbm.shape
    slots = n * CAP
    rows = sources * CAP
    turn = [lax.rem(pair + k, pairs) for k in range(pairs)]

    def remote(src, dst, k, o, r):
        return pltpu.make_async_remote_copy(
            src_ref=src, dst_ref=dst, send_sem=ssem.at[k], recv_sem=rsem.at[k],
            device_id={"expert": o, "replica": r}, device_id_type=pl.DeviceIdType.MESH,
        )

    def everyone(act):
        @pl.loop(1, n)
        def _(k):
            o = lax.rem(mo + lax.rem(k + n // 2 + 2 - 2 + n - 1, n - 1) + 1, n)
            for p in turn:
                act(o, p)

        for p in turn[1:]:
            act(mo, p)

    barrier = pltpu.get_barrier_semaphore()

    def hail(o, r):
        pl.semaphore_signal(
            barrier, inc=1, device_id={"expert": o, "replica": r},
            device_id_type=pl.DeviceIdType.MESH,
        )

    everyone(lambda o, p: hail(o, 2 * p + core))
    hail(mo, mate)

    loads = [
        pltpu.make_async_copy(src, dst, wsem.at[i])
        for i, (src, dst) in enumerate((
            (tok_hbm, tok_ref), (og_hbm, og_ref),
            (wg_hbm, wg_ref.at[core]), (wu_hbm, wu_ref.at[core]), (wd_hbm, wd_ref.at[core]),
        ))
    ]
    for load in loads:
        load.start()

    row = lax.broadcasted_iota(jnp.int32, (slots, block), 0)
    expert = row // (2 * CAP)
    place = row % CAP
    limit = jnp.zeros((slots, block), jnp.int32)
    for e in range(cap_ref.shape[0]):
        limit = jnp.where(expert == e, cap_ref[e], limit)
    named = jnp.zeros((slots, block), F32)
    weight = jnp.zeros((slots, block), F32)
    for k in range(ids_ref.shape[0]):
        hit = ids_ref[k : k + 1, :] == expert
        named = named + jnp.where(hit, 1.0, 0.0)
        weight = weight + jnp.where(hit, rw_ref[k : k + 1, :].astype(F32), 0.0)
    upper = jnp.where(
        lax.broadcasted_iota(jnp.int32, (block, block), 0)
        <= lax.broadcasted_iota(jnp.int32, (block, block), 1),
        1.0, 0.0,
    ).astype(BF16)
    ranks = dot(named.astype(BF16), upper, ((1,), (0,)))
    kept = (named > 0.0) & (ranks == (place + 1).astype(F32)) & (place < limit)
    picker = jnp.where(kept, 1.0, 0.0)
    slot_weight = jnp.sum(picker * weight, axis=1, keepdims=True)
    picker = picker.astype(BF16)
    pick_ref[...] = picker
    loads[0].wait()
    loads[1].wait()
    for r in range(reps):
        cols = pl.ds(r * dr, dr)
        picked = dot(picker, tok_ref[:, cols], ((1,), (0,)))
        scaled = dot(picker, og_ref[:, cols], ((1,), (0,))) * slot_weight
        send[:, r // 2, 0, r % 2] = picked.reshape(n, CAP, dr).astype(BF16)
        send[:, r // 2, 1, r % 2] = scaled.reshape(n, CAP, dr).astype(BF16)

    pl.semaphore_wait(barrier, sources)

    own = pltpu.make_async_copy(send.at[mo, pair], recv.at[:, :, me], lsem.at[0])
    own.start()
    everyone(
        lambda o, p: remote(send.at[o, p], recv.at[:, :, me], 0, o, 2 * p + core).start()
    )

    lent = [
        remote(src, dst.at[core], 2 + i, mo, mate)
        for i, (src, dst) in enumerate(((wg_hbm, wg_ref), (wu_hbm, wu_ref), (wd_hbm, wd_ref)))
    ]
    for copy in lent:
        copy.start()
    for load in loads[2:]:
        load.wait()
    own.wait()
    arrived = recv.at[:, :, pl.ds(0, sources - 1)]
    pltpu.make_async_copy(arrived, arrived, rsem.at[0]).wait()

    used = 5
    across = []
    for k in range(1, pairs):
        across.append(remote(recv.at[1], cots.at[core, pair], used, mo, 2 * turn[k] + core))
        across[-1].start()
        used += 1

    def flat(value):
        return value.astype(F32).reshape(rows, dr).astype(BF16)

    x0, x1 = flat(recv[0, 0]), flat(recv[0, 1])
    c0, c1 = flat(recv[1, 0]), flat(recv[1, 1])
    for copy in lent:
        copy.wait()
    wg, wu, wd = [wg_ref[0], wg_ref[1]], [wu_ref[0], wu_ref[1]], [wd_ref[0], wd_ref[1]]
    crossing = []
    for i in range(3):
        if i < 2:
            w = (wg, wu)[i]
            value = dot(x0, w[0], ((1,), (0,))) + dot(x1, w[1], ((1,), (0,)))
        else:
            value = dot(c0, wd[0], ((1,), (1,))) + dot(c1, wd[1], ((1,), (1,)))
        sums[i, pair] = value.astype(BF16)
        for k in range(1, pairs):
            crossing.append(
                remote(sums.at[i, pair], sums.at[i, pair], used, mo, 2 * turn[k] + core)
            )
            crossing[-1].start()
            used += 1
    for copy in crossing:
        copy.wait()

    def total(i):
        value = sums[i, 0].astype(F32)
        for k in range(1, pairs):
            value = value + sums[i, k].astype(F32)
        return value

    gate, up, back = total(0), total(1), total(2)
    sig = jax.nn.sigmoid(gate)
    act = gate * sig
    gate_back = (back * up * sig * (1.0 + gate * (1.0 - sig))).astype(BF16)
    up_back = (back * act).astype(BF16)
    for s in range(2):
        result = dot(gate_back, wg[s], ((1,), (1,))) + dot(up_back, wu[s], ((1,), (1,)))
        rsend[:, s] = result.reshape(sources, CAP, dr).astype(BF16)
    back_own = pltpu.make_async_copy(rsend.at[me], rrecv.at[mo, pair], lsem.at[1])
    back_own.start()
    everyone(
        lambda o, p: remote(
            rsend.at[o * pairs + p], rrecv.at[mo, pair], 1, o, 2 * p + core
        ).start()
    )

    grads[0, core] = gate_back
    grads[1, core] = up_back
    grads[2, core] = (act * up).astype(BF16)
    swaps = [
        remote(recv.at[0, 1 - core], xs.at[core], used, mo, mate),
        remote(grads.at[:, core], grads.at[:, core], used + 1, mo, mate),
        remote(recv.at[1], cots.at[core, pair], used + 2, mo, mate),
    ]
    for copy in swaps:
        copy.start()
    used += 3
    xs[core] = recv[0, core]
    for k in range(1, pairs):
        across[k - 1].wait()
        came = lax.rem(pair + pairs - k, pairs)
        swaps.append(remote(cots.at[core, came], cots.at[core, came], used, mo, mate))
        swaps[-1].start()
        used += 1
    cots[core, pair] = recv[1]
    for copy in swaps:
        copy.wait()

    inputs = xs[...].astype(F32).reshape(2 * rows, dr).astype(BF16)
    gg_ref[...] = dot(inputs, grads[0].reshape(2 * rows, half), ((0,), (0,))).astype(BF16)
    ug_ref[...] = dot(inputs, grads[1].reshape(2 * rows, half), ((0,), (0,))).astype(BF16)
    hidden = grads[2].reshape(2 * rows, half)
    for r in range(reps):
        c = cots[:, r // 2, r % 2].astype(F32).reshape(2 * rows, dr).astype(BF16)
        dg_ref[:, pl.ds(r * dr, dr)] = dot(hidden, c, ((0,), (0,))).astype(BF16)

    back_own.wait()
    returned = rsend.at[pl.ds(0, sources - 1)]
    pltpu.make_async_copy(returned, returned, rsem.at[1]).wait()
    for r in range(reps):
        parts = rrecv[:, r // 2, r % 2].astype(F32).reshape(slots, dr).astype(BF16)
        back_ref[:, pl.ds(r * dr, dr)] = parts
    pltpu.make_async_copy(arrived, arrived, ssem.at[0]).wait()
    pltpu.make_async_copy(returned, returned, ssem.at[1]).wait()


def finish(pick_ref, back_ref, gg_in, ug_in, dg_in, xg_out, gg_out, ug_out, dg_out, xg, sem):
    copies = [
        pltpu.make_async_copy(src, dst, sem.at[i])
        for i, (src, dst) in enumerate(
            ((dg_in, dg_out), (gg_in, gg_out), (ug_in, ug_out), (xg, xg_out))
        )
    ]
    for copy in copies[:3]:
        copy.start()
    xg[...] = dot(pick_ref[...], back_ref[...], ((0,), (0,))).astype(BF16)
    copies[3].start()
    for copy in copies:
        copy.wait()


def shards(n, reps, tokens, out_grad, expert_ids, route_weights, capacity, w_gate, w_up, w_down):
    block, width = tokens.shape
    dr, half = w_gate.shape[1:]
    pairs = reps // 2
    sources = n * pairs
    rows = sources * CAP
    sems = 8 + 5 * (pairs - 1)
    vmem = pl.BlockSpec(memory_space=pltpu.VMEM)
    hbm = pl.BlockSpec(memory_space=pl.ANY)
    shapes = ((block, width), (dr, half), (dr, half), (half, width))
    partial = pl.pallas_call(
        functools.partial(kernel, n, reps),
        out_shape=tuple(
            pltpu.VMEM(shape, BF16) for shape in ((n * CAP, block), (n * CAP, width), *shapes[1:])
        ),
        in_specs=[vmem, vmem, pl.BlockSpec(memory_space=pltpu.SMEM)] + [hbm] * 5,
        out_specs=(vmem,) * 5,
        scratch_shapes=[
            pltpu.VMEM((block, width), BF16),
            pltpu.VMEM((block, width), BF16),
            pltpu.VMEM((2, dr, half), BF16),
            pltpu.VMEM((2, dr, half), BF16),
            pltpu.VMEM((2, half, dr), BF16),
            pltpu.VMEM((n, pairs, 2, 2, CAP, dr), BF16),
            pltpu.VMEM((2, 2, sources, CAP, dr), BF16),
            pltpu.VMEM((2, sources, CAP, dr), BF16),
            pltpu.VMEM((2, pairs, 2, sources, CAP, dr), BF16),
            pltpu.VMEM((3, pairs, rows, half), BF16),
            pltpu.VMEM((3, 2, rows, half), BF16),
            pltpu.VMEM((sources, 2, CAP, dr), BF16),
            pltpu.VMEM((n, pairs, 2, CAP, dr), BF16),
            pltpu.SemaphoreType.DMA((5,)),
            pltpu.SemaphoreType.DMA((2,)),
            pltpu.SemaphoreType.DMA((sems,)),
            pltpu.SemaphoreType.DMA((sems,)),
        ],
        compiler_params=pltpu.CompilerParams(collective_id=0, has_side_effects=True),
    )(
        expert_ids.T, route_weights.T, capacity, tokens, out_grad,
        w_gate.reshape(dr, half), w_up.reshape(dr, half), w_down.reshape(half, dr),
    )
    x_grad, gate_grad, up_grad, down_grad = pl.pallas_call(
        finish,
        out_shape=tuple(jax.ShapeDtypeStruct(shape, BF16) for shape in shapes),
        in_specs=[vmem] * 5,
        out_specs=(hbm,) * 4,
        scratch_shapes=[pltpu.VMEM((block, width), BF16), pltpu.SemaphoreType.DMA((4,))],
    )(*(pltpu.with_memory_space_constraint(p, pltpu.VMEM) for p in partial))
    return x_grad, gate_grad[None], up_grad[None], down_grad[None]


def solution(mesh):
    return jax.shard_map(
        functools.partial(shards, mesh.shape["expert"], mesh.shape["replica"]),
        mesh=mesh,
        in_specs=(
            P(("expert", "replica"), None),
            P(("expert", "replica"), None),
            P(("expert", "replica"), None),
            P(("expert", "replica"), None),
            P(),
            P("expert", "replica", None),
            P("expert", "replica", None),
            P("expert", None, "replica"),
        ),
        out_specs=(
            P(("expert", "replica"), None),
            P("expert", "replica", None),
            P("expert", "replica", None),
            P("expert", None, None),
        ),
        check_vma=False,
    )
```
